256 devices in a mesh: seg: 8 (over z), src: 32 (over x, y, core).
Axes of the slice: x: 4, y: 4, z: 8, core: 2. Of those that a mesh axis runs over, the one named last changes fastest.
Arguments:
- attitude_partials: bfloat16 [8, 4, 524288], P('seg', None, 'src'), may hold values from -0.59765625 to 0.59765625
- scan_phase: float32 [8, 524288], P('seg', 'src'), may hold values from 0 to 1
- huber_weight: float32 [8, 524288], P('seg', 'src'), may hold values from 0.1 to 1
- residual: float32 [8, 524288], P('seg', 'src')
- knot_offset: int32 [8, 524288], P('seg', 'src'), may hold values from 0 to 124
- detector_index: int32 [8, 524288], P('seg', 'src'), may hold values from 0 to 61
- calibration_partials: bfloat16 [8, 4, 524288], P('seg', None, 'src'), may hold values from 0.5 to 1.5
- source_index: int32 [8, 524288], P('seg', 'src'), may hold values from 0 to 127
- source_partials: bfloat16 [8, 5, 524288], P('seg', None, 'src')
- send_counts: int32 [8, 32, 32], P('seg', 'src'), may hold values from 0 to 8, as said below
Outputs:
- attitude_step: float32 [8, 4, 4096], P('seg', None, 'src')
- calibration_step: float32 [8, 4, 62], P('seg')
- source_step: float32 [5, 4096], P(None, 'src')
- updated_residual: float32 [8, 524288], P('seg', 'src')
The draws below stay inside these ranges and needn't reach their ends.
Inputs may be any that keep to these rules, and one draw needn't show every extreme that they name: Each row send_counts[s, q, :] sums to 128; the blocks of a shard are stored in order of owner; in every segment one owner receives exactly 8 blocks from every shard.
All inputs are finite; a program needn't handle non-finite values.
Results may differ from the reference program's by a relative error of at most 0.0003.
Values sent between devices are 32-bit elements; how exact they have to be, the bound alone decides.
A program may use at most 64 MiB of HBM per device.

```python
import jax
import jax.numpy as jnp
import numpy as np
from jax import lax

QC = 4
SP = 5
CALP = 4
CCDS = 62
BSIZE = 128
ITERS = 6
KN_DEV = 128
BLK_DEV = 128
S_DEV = 128
SEGMENTS = 8
SHARDS = 32
TR_DEV = 16384
TRANSITS = 524288
KNOTS = 4096
SOURCES = 4096
CAP = 8


def sample_transits(key):
    detectors = jax.random.randint(jax.random.fold_in(key, 11), (SEGMENTS, TRANSITS), 0, CCDS, dtype=jnp.int32)
    sources = jax.random.randint(jax.random.fold_in(key, 12), (SEGMENTS, TRANSITS), 0, S_DEV, dtype=jnp.int32)
    source_terms = jax.random.normal(jax.random.fold_in(key, 13), (SEGMENTS, SP, TRANSITS), jnp.float32)
    ccd_bias = jax.random.normal(jax.random.fold_in(key, 14), (SEGMENTS, CCDS), jnp.float32)
    source_truth = jax.random.normal(jax.random.fold_in(key, 15), (SOURCES, SP), jnp.float32)
    shard_index = jnp.arange(TRANSITS, dtype=jnp.int32) // TR_DEV
    global_source = shard_index[None, :] * S_DEV + sources
    picked = jnp.take(source_truth, global_source, axis=0)
    signal = jnp.sum(jnp.moveaxis(picked, -1, 1) * source_terms, axis=1)
    bias_term = jnp.take_along_axis(ccd_bias, detectors, axis=1)
    return (detectors, sources, source_terms, signal, bias_term)


def draw_residual(key, part):
    detectors, sources, source_terms, signal, bias_term = sample_transits(key)
    noise_term = jax.random.normal(jax.random.fold_in(key, 16), (SEGMENTS, TRANSITS), jnp.float32)
    return noise_term + bias_term + signal


def draw_detector_index(key, part):
    return sample_transits(key)[0]


def draw_source_index(key, part):
    return sample_transits(key)[1]


def draw_source_partials(key, part):
    return sample_transits(key)[2].astype(jnp.bfloat16)


def draw_send_counts(key, part):
    busiest = jax.random.randint(jax.random.fold_in(key, 21), (SEGMENTS,), 0, SHARDS, dtype=jnp.int32)
    remaining = BLK_DEV - CAP
    targets = jnp.arange(SHARDS, dtype=jnp.int32)

    def one_row(row_number):
        busiest_peer = busiest[row_number // SHARDS]
        row_key = jax.random.fold_in(jax.random.fold_in(key, 22), row_number)
        shuffled = jax.random.permutation(row_key, (SHARDS - 1) * CAP)[:remaining].astype(jnp.int32)
        other_peer = shuffled // CAP
        target = other_peer + (other_peer >= busiest_peer).astype(jnp.int32)
        block_loads = jnp.sum((target[:, None] == targets[None, :]).astype(jnp.int32), axis=0)
        return block_loads + CAP * (targets == busiest_peer).astype(jnp.int32)
    all_rows = jax.vmap(one_row)(jnp.arange(SEGMENTS * SHARDS, dtype=jnp.int32))
    return all_rows.reshape(SEGMENTS, SHARDS, SHARDS)


def plant(values, stream_key, least, largest):
    longest = values.shape.index(max(values.shape))
    spots = []
    for shift in (0, 1):
        where = [jax.random.randint(jax.random.fold_in(stream_key, axis), (), 0, length) for axis, length in enumerate(values.shape)]
        where[longest] = (where[longest] + shift) % values.shape[longest]
        spots.append(tuple(where))
    return values.at[spots[0]].set(least).at[spots[1]].set(largest)


def shard_levels(stream_key, shape, cuts, smallest, high):
    level = 1.0
    for position, parts in cuts:
        draws = jax.random.uniform(jax.random.fold_in(jax.random.fold_in(stream_key, 6), position), (parts,), jnp.float32, smallest / len(cuts), high / len(cuts))
        level = level * jnp.repeat(jnp.exp(draws), shape[position] // parts).reshape((-1,) + (1,) * (len(shape) - 1 - position))
    return level


def scatter_about(stream_key, shape, scale, most, cuts=(), kind=jnp.bfloat16):
    entries = jax.random.normal(stream_key, shape, jnp.float32) * scale
    if len(cuts) > 0:
        entries = shard_levels(stream_key, shape, cuts, -0.22, 0.18) * entries
    return jnp.clip(entries, min=-most, max=most).astype(kind)


def setup_inputs(seed: int = 0) -> dict:
    streams_of = jax.random.split(jax.random.key(seed), 11)
    attitude_partials = scatter_about(streams_of[0], (SEGMENTS, QC, TRANSITS), 0.1, 0.59765625, ((0, 8), (2, 32)))
    scan_phase = jnp.clip(1.0 * jax.random.uniform(streams_of[1], (SEGMENTS, TRANSITS), jnp.float32) ** shard_levels(streams_of[1], (SEGMENTS, TRANSITS), ((0, 8), (1, 32)), -0.2, 0.2), 0.0, 1.0)
    huber_weight = jnp.clip(0.1 + 0.9 * jax.random.uniform(streams_of[2], (SEGMENTS, TRANSITS), jnp.float32) ** shard_levels(streams_of[2], (SEGMENTS, TRANSITS), ((0, 8), (1, 32)), -0.2, 0.2), 0.1, 1.0)
    residual = draw_residual(jax.random.fold_in(streams_of[10], 71), 0)
    knot_offset = plant(jax.random.randint(streams_of[4], (SEGMENTS, TRANSITS), 0, KN_DEV - 3), jax.random.fold_in(streams_of[4], 1), 0, (KN_DEV - 3) - 1).astype(jnp.int32)
    detector_index = draw_detector_index(jax.random.fold_in(streams_of[10], 71), 0)
    calibration_partials = jnp.clip(0.5 + 1.0 * jax.random.uniform(streams_of[6], (SEGMENTS, CALP, TRANSITS), jnp.float32) ** shard_levels(streams_of[6], (SEGMENTS, CALP, TRANSITS), ((0, 8), (2, 32)), -0.2, 0.2), 0.5, 1.5).astype(jnp.bfloat16)
    source_index = draw_source_index(jax.random.fold_in(streams_of[10], 71), 0)
    source_partials = draw_source_partials(jax.random.fold_in(streams_of[10], 71), 0)
    send_counts = draw_send_counts(jax.random.fold_in(streams_of[10], 71), 0)
    return dict(attitude_partials=attitude_partials, scan_phase=scan_phase, huber_weight=huber_weight, residual=residual, knot_offset=knot_offset, detector_index=detector_index, calibration_partials=calibration_partials, source_index=source_index, source_partials=source_partials, send_counts=send_counts)


highest = lax.Precision.HIGHEST
attitude_prior = 0.5
pair_left = np.array([0, 1, 2, 3, 0, 1, 2, 0, 1, 0])
pair_right = np.array([0, 1, 2, 3, 1, 2, 3, 2, 3, 3])
pair_start = (0, 4, 7, 9)
group_blocks = 16


def spline_basis(phases):
    rest = 1.0 - phases
    square = phases * phases
    cubed = square * phases
    return jnp.stack([rest * rest * rest / 6.0, (3.0 * cubed - 6.0 * square + 4.0) / 6.0,
                      (-3.0 * cubed + 3.0 * square + 3.0 * phases + 1.0) / 6.0, cubed / 6.0], 0)


def row_features(partials, phases, weight, residual_now):
    columns = phases.shape[-1]
    spline = spline_basis(phases)
    basis_pairs = spline[pair_left] * spline[pair_right]
    outer_partials = (partials[:, None, :] * partials[None, :, :]).reshape(16, columns)
    products = ((weight * basis_pairs)[:, None, :] * outer_partials[None]).reshape(160, columns)
    right_terms = ((weight * residual_now * spline)[:, None, :] * partials[None]).reshape(16, columns)
    return jnp.concatenate([products, right_terms], 0), spline


def shift_knots(values, shift_amount):
    if shift_amount == 0:
        return values
    padding = jnp.zeros(values.shape[:-1] + (abs(shift_amount),), values.dtype)
    if shift_amount > 0:
        return jnp.concatenate([padding, values[..., :-shift_amount]], axis=-1)
    return jnp.concatenate([values[..., -shift_amount:], padding], axis=-1)


def normal_system(totals):
    span_knots = totals.shape[-1]
    products = totals[:160].reshape(10, 4, 4, span_knots)
    right_terms = totals[160:].reshape(4, 4, span_knots)
    blocks = []
    for d in range(4):
        summed = products[pair_start[d]]
        for i in range(1, 4 - d):
            summed = summed + shift_knots(products[pair_start[d] + i], i)
        blocks.append(summed)
    right_side = right_terms[0]
    for i in range(1, 4):
        right_side = right_side + shift_knots(right_terms[i], i)
    return blocks, right_side


def apply_normal(blocks, values):
    result = attitude_prior * values + jnp.einsum("jlk,lk->jk", blocks[0], values, precision=highest)
    for d in range(1, 4):
        result = result + jnp.einsum("jlk,lk->jk", blocks[d], shift_knots(values, -d), precision=highest)
        result = result + shift_knots(jnp.einsum("jlk,jk->lk", blocks[d], values, precision=highest), d)
    return result


def solve_attitude(blocks, right_side):
    diagonal = jnp.stack([blocks[0][j, j] for j in range(4)], 0) + attitude_prior
    solution = jnp.zeros_like(right_side)
    remaining = right_side
    scaled = remaining / diagonal
    direction = scaled
    precond_norm = jnp.sum(remaining * scaled)
    for step_index in range(ITERS):
        product_image = apply_normal(blocks, direction)
        step_length = precond_norm / jnp.sum(direction * product_image)
        solution = solution + step_length * direction
        remaining = remaining - step_length * product_image
        scaled = remaining / diagonal
        norm_next = jnp.sum(remaining * scaled)
        direction = scaled + (norm_next / precond_norm) * direction
        precond_norm = norm_next
    return solution


def knot_table(solution):
    shifted = [shift_knots(solution, -i) for i in range(4)]
    stacked = jnp.stack(shifted, axis=-3)
    return stacked.reshape(solution.shape[:-2] + (16, solution.shape[-1]))


def correction(spline, partials, values_at):
    grid = values_at.reshape((4, 4) + values_at.shape[1:])
    return jnp.sum(spline[:, None] * partials[None] * grid, axis=(0, 1))


def reference(attitude_partials, scan_phase, huber_weight, residual, knot_offset, detector_index,
              calibration_partials, source_index, source_partials, send_counts):
    group_rows = group_blocks * BSIZE

    def one_segment(pieces):
        partials, phases, weight, residual_now, offsets, detectors, calibration, sources, source_terms, counts = pieces
        partials = partials.astype(jnp.float32)
        calibration = calibration.astype(jnp.float32)
        source_terms = source_terms.astype(jnp.float32)
        run_ends = jnp.cumsum(counts, axis=1)
        block_ids = jnp.arange(BLK_DEV, dtype=jnp.int32)
        block_owner = jnp.sum((run_ends[:, None, :] <= block_ids[None, :, None]).astype(jnp.int32), axis=2)
        owners = jnp.broadcast_to(block_owner[:, :, None], (SHARDS, BLK_DEV, BSIZE)).reshape(TRANSITS)
        knot_index = owners * KN_DEV + offsets

        def add_group(totals, group_index):
            first_row = group_index * group_rows

            def slice_group(array):
                return lax.dynamic_slice_in_dim(array, first_row, group_rows, array.ndim - 1)

            features, unused = row_features(slice_group(partials), slice_group(phases),
                                            slice_group(weight), slice_group(residual_now))
            summed = jax.ops.segment_sum(features.T, slice_group(knot_index), num_segments=KNOTS)
            return totals + summed, None

        totals, unused = lax.scan(add_group, jnp.zeros((KNOTS, 176), jnp.float32),
                                  jnp.arange(TRANSITS // group_rows, dtype=jnp.int32))
        totals = totals.reshape(SHARDS, KN_DEV, 176).transpose(0, 2, 1)

        def owner_solve(owned):
            blocks, right_side = normal_system(owned)
            return solve_attitude(blocks, right_side)

        solutions = jax.vmap(owner_solve)(totals)
        table_all = knot_table(solutions).transpose(1, 0, 2).reshape(16, KNOTS)
        values_at = jnp.take(table_all, knot_index, axis=1)
        spline = spline_basis(phases)
        updated = residual_now - correction(spline, partials, values_at)
        calib_features = jnp.concatenate([weight * updated * calibration, weight * calibration * calibration], 0)
        calib_totals = jax.ops.segment_sum(calib_features.T, detectors, num_segments=CCDS)
        calib_result = (calib_totals[:, :CALP] / (1.0 + calib_totals[:, CALP:])).T
        shard_index = jnp.arange(TRANSITS, dtype=jnp.int32) // TR_DEV
        global_source = shard_index * S_DEV + sources
        source_features = jnp.concatenate([weight * updated * source_terms, weight * source_terms * source_terms], 0)
        source_totals = jax.ops.segment_sum(source_features.T, global_source, num_segments=SOURCES)
        attitude = solutions.transpose(1, 0, 2).reshape(QC, KNOTS)
        return attitude, calib_result, source_totals, updated

    attitude, calib_result, source_totals, updated = lax.map(
        one_segment, (attitude_partials, scan_phase, huber_weight, residual, knot_offset, detector_index,
                      calibration_partials, source_index, source_partials, send_counts))
    summed = jnp.sum(source_totals, axis=0)
    source_result = (summed[:, :SP] / (1.0 + summed[:, SP:])).T
    return attitude, calib_result, source_result, updated
```

```python
import functools

import jax
import jax.numpy as jnp
from jax import lax
from jax.experimental import pallas as pl
from jax.experimental.pallas import tpu as pltpu
from jax.sharding import PartitionSpec as P

SP = 5
CALP = 4
CCDS = 62
BSIZE = 128
ITERS = 6
LANES = 128
GROUP = 8
PACKED = 48
attitude_prior = 0.5
f32 = jnp.float32
bf16 = jnp.bfloat16
MESH = pl.DeviceIdType.MESH
VMEM = pltpu.VMEM
nt = (((1,), (1,)), ((), ()))

pairs = [(d, i) for d in range(4) for i in range(4 - d)]


def spline_basis(u):
    rest = 1.0 - u
    square = u * u
    cubed = square * u
    return [
        rest * rest * rest / 6.0,
        (3.0 * cubed - 6.0 * square + 4.0) / 6.0,
        (-3.0 * cubed + 3.0 * square + 3.0 * u + 1.0) / 6.0,
        cubed / 6.0,
    ]


def row_ids():
    return lax.broadcasted_iota(jnp.int32, (8, LANES), 0)


def split_two(x):
    high = x.astype(bf16)
    return high, (x - high.astype(f32)).astype(bf16)


def spread(ref, row, rows=8):
    return jnp.broadcast_to(ref[pl.ds(row, 1), :], (rows, LANES))


def one_hot(index_rows, count):
    ids = lax.broadcasted_iota(jnp.int32, (count, LANES), 0).astype(f32).astype(bf16)
    picked = jnp.broadcast_to(index_rows, (count, LANES)).astype(bf16)
    return jnp.where(picked == ids, jnp.ones((), bf16), jnp.zeros((), bf16))


def fill_owners(counts_ref, owner_ref, owners, blocks, capacity):
    start = jnp.int32(0)
    for o in range(owners):
        for c in range(capacity):
            owner_ref[start + c] = jnp.int32(o)
        start = start + counts_ref[0, o]


def twice(x):
    return jnp.concatenate([x, x], axis=0)


def assemble_kernel(
    owners, capacity, counts_ref, part_ref, phase_ref, weight_ref, resid_ref, offset_ref,
    out_ref, owner_ref, rows_ref, acc_ref,
):
    blocks = phase_ref.shape[0]
    stride = 64
    fill_owners(counts_ref, owner_ref, owners, blocks, capacity)
    acc_ref[...] = jnp.zeros_like(acc_ref)
    rows_ref[...] = jnp.zeros_like(rows_ref)
    low = row_ids() < 4

    def group_step(group, carry):
        base = pl.multiple_of(group * GROUP, GROUP)
        here = pl.ds(base, GROUP)
        spline = spline_basis(phase_ref[here, :])
        weight = weight_ref[here, :]
        weighted = [weight * s for s in spline]
        resid = resid_ref[here, :]

        def put(row, value):
            rows_ref[pl.ds(row, GROUP, stride=stride), :] = value

        for p, (d, i) in enumerate(pairs):
            value = weighted[i] * spline[i + d]
            put(p, value)
            put(16 + 8 * i + 2 * d, value)
            put(16 + 8 * i + 2 * d + 1, value)
        put(10, offset_ref[here, :].astype(f32))
        for i in range(4):
            value = weighted[i] * resid
            for j in range(4):
                put(48 + 4 * i + j, value)
        for q in range(GROUP):
            first = q * stride
            lanes = pl.ds(pl.multiple_of((base + q) * BSIZE, BSIZE), BSIZE)
            a8 = twice(part_ref[0, :, lanes].astype(f32))
            main = a8 * jnp.where(low, a8, pltpu.roll(a8, 7, 0))
            cross = a8 * pltpu.roll(a8, 6, 0)
            features = [main * spread(rows_ref, first + p) for p in range(10)]
            features += [cross * rows_ref[pl.ds(first + 16 + 8 * i, 8), :] for i in range(4)]
            features += [a8 * rows_ref[pl.ds(first + 48 + 8 * h, 8), :] for h in range(2)]
            high, rest = split_two(jnp.concatenate(features, axis=0))
            hot = one_hot(rows_ref[pl.ds(first + 10, 1), :], LANES)
            summed = lax.dot_general(
                jnp.concatenate([high, rest], axis=1), jnp.concatenate([hot, hot], axis=1),
                nt, preferred_element_type=f32,
            )
            owner = owner_ref[base + q]
            acc_ref[owner] = acc_ref[owner] + summed
        return carry

    lax.fori_loop(0, blocks // GROUP, group_step, 0)

    def pack_chip(chip, carry):
        for core in range(2):
            tiles = acc_ref.at[2 * chip + core]

            def shifted(t, i):
                tile = tiles[pl.ds(8 * t, 8), :]
                return tile if i == 0 else pltpu.roll(tile, i, 1)

            for d in range(4):
                total = None
                for p, (pd, i) in enumerate(pairs):
                    if pd == d:
                        term = shifted(p, i)
                        total = term if total is None else total + term
                out_ref[core, chip, pl.ds(8 * d, 8), :] = total
            out_ref[core, chip, pl.ds(32, 8), :] = (
                (shifted(10, 0) + shifted(11, 1)) + (shifted(12, 2) + shifted(13, 3))
            )
            out_ref[core, chip, pl.ds(40, 8), :] = jnp.where(
                low, shifted(14, 0), shifted(14, 1)
            ) + jnp.where(low, shifted(15, 2), shifted(15, 3))
        return carry

    lax.fori_loop(0, owners // 2, pack_chip, 0)


def total_of(x):
    return jnp.sum(jnp.sum(x, axis=1, keepdims=True), axis=0, keepdims=True)


def solve_owner(tiles):
    low = row_ids() < 4
    right_side = tiles[5] + pltpu.roll(tiles[5], 4, 0)
    cross = tiles[4]
    coefficients = []
    for d in range(4):
        first = tiles[d]
        pair_now = cross[2 * d : 2 * d + 2]
        second = jnp.concatenate([pair_now, pair_now, first[7:8], first[4:7]], axis=0)
        if d == 0:
            first = jnp.where(low, first + attitude_prior, first)
            coefficients.append((0, first, second))
            diagonal = jnp.where(low, first, pltpu.roll(first, 4, 0))
        else:
            coefficients.append((d, first, second))
            coefficients.append((-d, pltpu.roll(first, d, 1), pltpu.roll(second, d, 1)))

    def apply_normal(p):
        near = jnp.where(low, p, pltpu.roll(p, 7, 0))
        far = jnp.where(low, pltpu.roll(p, 6, 0), pltpu.roll(p, 5, 0))
        terms = []
        for d, first, second in coefficients:
            if d == 0:
                terms.append(first * near + second * far)
            else:
                shift = (LANES - d) % LANES
                terms.append(first * pltpu.roll(near, shift, 1) + second * pltpu.roll(far, shift, 1))
        result = ((terms[0] + terms[1]) + (terms[2] + terms[3])) + (
            (terms[4] + terms[5]) + terms[6]
        )
        return result + pltpu.roll(result, 4, 0)

    step = jnp.zeros_like(right_side)
    remaining = right_side
    scaled = remaining / diagonal
    direction = scaled
    norm = total_of(remaining * scaled)
    for iteration in range(ITERS):
        image = apply_normal(direction)
        length = norm / total_of(direction * image)
        step = step + length * direction
        if iteration + 1 < ITERS:
            remaining = remaining - length * image
            scaled = remaining / diagonal
            norm_next = total_of(remaining * scaled)
            direction = scaled + norm_next / norm * direction
            norm = norm_next
    return step


def loop(lower, upper, step):
    def run(k, carry):
        step(k)
        return carry

    lax.fori_loop(lower, upper, run, 0)


def exchange_kernel(
    owners, parts_ref, out_ref, got_pair, mine, got_chip, got_step,
    pair_send, pair_recv, chip_send, chip_recv, step_send, step_recv,
):
    chips = owners // 2
    me = lax.axis_index("src")
    core = lax.rem(me, 2)
    chip = me // 2
    partner = me + 1 - 2 * core
    barrier = pltpu.get_barrier_semaphore()

    def greet(k):
        pl.semaphore_signal(
            barrier, inc=1, device_id={"src": lax.rem(me + k, owners)}, device_id_type=MESH
        )

    loop(1, owners, greet)
    pl.semaphore_wait(barrier, owners - 1)

    def pair_copy(k):
        target_chip = lax.rem(chip + k, chips)
        return pltpu.make_async_remote_copy(
            src_ref=parts_ref.at[1 - core, target_chip], dst_ref=got_pair.at[k],
            send_sem=pair_send.at[k], recv_sem=pair_recv.at[k],
            device_id={"src": partner}, device_id_type=MESH,
        )

    def chip_copy(k):
        return pltpu.make_async_remote_copy(
            src_ref=mine.at[k], dst_ref=got_chip.at[k],
            send_sem=chip_send.at[k], recv_sem=chip_recv.at[k],
            device_id={"src": 2 * lax.rem(chip + k, chips) + core}, device_id_type=MESH,
        )

    loop(1, chips, lambda k: pair_copy(k).start())
    pair_copy(0).start()

    def add_pair(k):
        pair_copy(k).wait_recv()
        mine[k] = parts_ref[core, lax.rem(chip + k, chips)] + got_pair[k]

    add_pair(1)

    def add_and_send(k):
        add_pair(k)
        chip_copy(k - 1).start()

    loop(2, chips, add_and_send)
    add_pair(0)
    chip_copy(chips - 1).start()

    def gather(k, total):
        chip_copy(k).wait_recv()
        return total + got_chip[k]

    total = lax.fori_loop(1, chips, gather, mine[0])
    step = solve_owner([total[8 * t : 8 * t + 8] for t in range(PACKED // 8)])
    got_step[me] = step[0:4]

    def step_copy(k, slot):
        return pltpu.make_async_remote_copy(
            src_ref=got_step.at[slot], dst_ref=got_step.at[slot],
            send_sem=step_send.at[k], recv_sem=step_recv.at[slot],
            device_id={"src": lax.rem(me + k, owners)}, device_id_type=MESH,
        )

    loop(1, owners, lambda k: step_copy(k, me).start())

    def drain(k):
        pair_copy(k).wait_send()
        chip_copy(k).wait_send()

    loop(1, chips, drain)
    pair_copy(0).wait_send()
    loop(1, owners, lambda k: step_copy(k, lax.rem(me + k, owners)).wait_recv())
    out_ref[...] = got_step[...]
    loop(1, owners, lambda k: step_copy(k, me).wait_send())


def correct_kernel(
    owners, owner_ref, steps_ref, part_ref, phase_ref, weight_ref, resid_ref, offset_ref,
    detector_ref, calib_ref, source_ref, sterm_ref,
    updated_ref, calsum_ref, srcsum_ref, rows_ref, table_ref, acc_ref,
):
    blocks = phase_ref.shape[0]
    stride = 24
    rows = row_ids()
    low = rows < 4

    def make_table(o, carry):
        x8 = twice(steps_ref[o])
        table = jnp.concatenate(
            [
                jnp.where(low, x8, pltpu.roll(x8, LANES - 1, 1)),
                jnp.where(low, pltpu.roll(x8, LANES - 2, 1), pltpu.roll(x8, LANES - 3, 1)),
            ],
            axis=0,
        )
        high, rest = split_two(table)
        table_ref[o] = jnp.concatenate([high, rest], axis=0)
        return carry

    lax.fori_loop(0, owners, make_table, 0)
    acc_ref[...] = jnp.zeros_like(acc_ref)

    def group_step(group, carry):
        base = pl.multiple_of(group * GROUP, GROUP)
        here = pl.ds(base, GROUP)
        spline = spline_basis(phase_ref[here, :])

        def put(row, value):
            rows_ref[pl.ds(row, GROUP, stride=stride), :] = value

        put(0, offset_ref[here, :].astype(f32))
        put(1, source_ref[here, :].astype(f32))
        put(2, detector_ref[here, :].astype(f32))
        put(3, weight_ref[here, :])
        put(4, resid_ref[here, :])
        for i in range(4):
            for j in range(4):
                put(8 + 4 * i + j, spline[i])
        lefts = []
        rights = []
        for q in range(GROUP):
            first = q * stride
            lanes = pl.ds(pl.multiple_of((base + q) * BSIZE, BSIZE), BSIZE)
            a8 = twice(part_ref[0, :, lanes].astype(f32))
            hot = one_hot(rows_ref[pl.ds(first, 1), :], LANES)
            values = jnp.dot(table_ref[owner_ref[base + q]], hot, preferred_element_type=f32)
            term = a8 * (
                rows_ref[pl.ds(first + 8, 8), :] * (values[0:8] + values[16:24])
                + rows_ref[pl.ds(first + 16, 8), :] * (values[8:16] + values[24:32])
            )
            term = term + pltpu.roll(term, 4, 0)
            term = term + pltpu.roll(term, 2, 0)
            term = term + pltpu.roll(term, 1, 0)
            updated = spread(rows_ref, first + 4) - term
            updated_ref[pl.ds(base + q, 1), :] = updated[0:1]
            weight = spread(rows_ref, first + 3)
            pull = weight * updated
            sterm = sterm_ref[0, :, lanes].astype(f32)
            eight = jnp.concatenate([sterm[0:4], calib_ref[0, :, lanes].astype(f32)], axis=0)
            fifth = jnp.broadcast_to(sterm[4:5], (8, LANES))
            last = jnp.where(rows == 0, pull, jnp.where(rows == 1, weight * fifth, 0.0)) * fifth
            high, rest = split_two(
                jnp.concatenate([pull * eight, weight * eight * eight, last], axis=0)
            )
            lefts.append(jnp.concatenate([high.astype(f32), rest.astype(f32)], axis=0).astype(bf16))
            rights.append(
                jnp.concatenate(
                    [
                        one_hot(rows_ref[pl.ds(first + 1, 1), :], LANES),
                        one_hot(rows_ref[pl.ds(first + 2, 1), :], LANES),
                    ],
                    axis=0,
                )
            )
        acc_ref[...] += lax.dot_general(
            jnp.concatenate(lefts, axis=1), jnp.concatenate(rights, axis=1), nt,
            preferred_element_type=f32,
        )
        return carry

    lax.fori_loop(0, blocks // GROUP, group_step, 0)
    sums = acc_ref[0:24] + acc_ref[24:48]
    for_source = sums[:, 0:LANES]
    for_calib = sums[:, LANES : 2 * LANES]
    srcsum_ref[0:8] = jnp.concatenate([for_source[0:4], for_source[8:12]], axis=0)
    srcsum_ref[8:16] = for_source[16:24]
    lane = lax.broadcasted_iota(jnp.int32, (4, LANES), 1)
    calsum_ref[...] = jnp.where(lane < 64, for_calib[4:8], pltpu.roll(for_calib, 64, 1)[12:16])


def sums_kernel(
    owners, segments, calsum_ref, srcsum_ref, calib_ref, source_ref, got_cal, got_src,
    cal_send, cal_recv, src_send, src_recv,
):
    me = lax.axis_index("src")
    segment = lax.axis_index("seg")
    barrier = pltpu.get_barrier_semaphore()

    def greet_src(k):
        pl.semaphore_signal(
            barrier, inc=1, device_id={"src": lax.rem(me + k, owners)}, device_id_type=MESH
        )

    def greet_seg(k):
        pl.semaphore_signal(
            barrier, inc=1, device_id={"seg": lax.rem(segment + k, segments)}, device_id_type=MESH
        )

    loop(1, segments, greet_seg)
    loop(1, owners, greet_src)
    pl.semaphore_wait(barrier, owners + segments - 2)

    def src_copy(k, slot):
        return pltpu.make_async_remote_copy(
            src_ref=srcsum_ref, dst_ref=got_src.at[slot],
            send_sem=src_send.at[k], recv_sem=src_recv.at[slot],
            device_id={"seg": lax.rem(segment + k, segments)}, device_id_type=MESH,
        )

    def cal_copy(k, slot):
        return pltpu.make_async_remote_copy(
            src_ref=calsum_ref, dst_ref=got_cal.at[slot],
            send_sem=cal_send.at[k], recv_sem=cal_recv.at[slot],
            device_id={"src": lax.rem(me + k, owners)}, device_id_type=MESH,
        )

    loop(1, segments, lambda k: src_copy(k, segment).start())
    loop(1, owners, lambda k: cal_copy(k, me).start())
    got_src[segment] = srcsum_ref[...]
    got_cal[me] = calsum_ref[...]
    loop(1, segments, lambda k: src_copy(k, lax.rem(segment + k, segments)).wait_recv())
    total = got_src[0]
    for k in range(1, segments):
        total = total + got_src[k]
    source_ref[0:4] = total[0:4] / (1.0 + total[4:8])
    source_ref[4:5] = total[8:9] / (1.0 + total[9:10])
    loop(1, owners, lambda k: cal_copy(k, lax.rem(me + k, owners)).wait_recv())
    total = got_cal[0]
    for k in range(1, owners):
        total = total + got_cal[k]
    result = total / (1.0 + pltpu.roll(total, 64, 1))
    calib_ref[...] = result[:, 0:CCDS]
    loop(1, segments, lambda k: src_copy(k, segment).wait_send())
    loop(1, owners, lambda k: cal_copy(k, me).wait_send())


def body(
    attitude_partials, scan_phase, huber_weight, residual, knot_offset, detector_index,
    calibration_partials, source_index, source_partials, send_counts,
):
    owners = lax.axis_size("src")
    segments = lax.axis_size("seg")
    blocks = scan_phase.shape[1] // BSIZE
    capacity = 2 * blocks // owners
    chips = owners // 2
    spec = pl.BlockSpec(memory_space=VMEM)
    scalars = pl.BlockSpec(memory_space=pltpu.SMEM)
    shape = jax.ShapeDtypeStruct
    dma = pltpu.SemaphoreType.DMA

    def by_block(x):
        return x.reshape(blocks, BSIZE)

    phase, weight, resid, offset = map(by_block, (scan_phase, huber_weight, residual, knot_offset))
    parts, owner_of = pl.pallas_call(
        functools.partial(assemble_kernel, owners, capacity),
        out_shape=(shape((2, chips, PACKED, LANES), f32), shape((blocks + capacity,), jnp.int32)),
        in_specs=[scalars] + [spec] * 5,
        out_specs=(spec, scalars),
        scratch_shapes=[VMEM((GROUP * 64, LANES), f32), VMEM((owners, LANES, LANES), f32)],
        name="assemble",
    )(send_counts.reshape(1, owners), attitude_partials, phase, weight, resid, offset)
    steps = pl.pallas_call(
        functools.partial(exchange_kernel, owners),
        out_shape=shape((owners, 4, LANES), f32),
        in_specs=[spec],
        out_specs=spec,
        scratch_shapes=[VMEM((chips, PACKED, LANES), f32)] * 3
        + [VMEM((owners, 4, LANES), f32)]
        + [dma((chips,))] * 4
        + [dma((owners,))] * 2,
        compiler_params=pltpu.CompilerParams(collective_id=0, has_side_effects=True),
        name="exchange",
    )(parts)
    updated, calsum, srcsum = pl.pallas_call(
        functools.partial(correct_kernel, owners),
        out_shape=(shape((blocks, BSIZE), f32), shape((4, LANES), f32), shape((16, LANES), f32)),
        in_specs=[scalars] + [spec] * 10,
        out_specs=(spec, spec, spec),
        scratch_shapes=[
            VMEM((GROUP * 24, LANES), f32), VMEM((owners, 32, LANES), bf16),
            VMEM((48, 2 * LANES), f32),
        ],
        name="correct",
    )(
        owner_of, steps, attitude_partials, phase, weight, resid, offset,
        by_block(detector_index), calibration_partials, by_block(source_index), source_partials,
    )
    calib, source = pl.pallas_call(
        functools.partial(sums_kernel, owners, segments),
        out_shape=(shape((CALP, CCDS), f32), shape((SP, LANES), f32)),
        in_specs=[spec] * 2,
        out_specs=(spec, spec),
        scratch_shapes=[
            VMEM((owners, 4, LANES), f32), VMEM((segments, 16, LANES), f32),
            dma((owners,)), dma((owners,)), dma((segments,)), dma((segments,)),
        ],
        compiler_params=pltpu.CompilerParams(collective_id=1, has_side_effects=True),
        name="sums",
    )(calsum, srcsum)
    mine = lax.dynamic_index_in_dim(steps, lax.axis_index("src"), 0, keepdims=True)
    return (mine, calib[None], source, updated.reshape(1, blocks * BSIZE))


def solution(mesh):
    return jax.shard_map(
        body,
        mesh=mesh,
        in_specs=(
            P("seg", None, "src"),
            P("seg", "src"),
            P("seg", "src"),
            P("seg", "src"),
            P("seg", "src"),
            P("seg", "src"),
            P("seg", None, "src"),
            P("seg", "src"),
            P("seg", None, "src"),
            P("seg", "src", None),
        ),
        out_specs=(P("seg", None, "src"), P("seg", None, None), P(None, "src"), P("seg", "src")),
        check_vma=False,
    )
```

```python
import functools

import jax
import jax.numpy as jnp
from jax import lax
from jax.experimental import pallas as pl
from jax.experimental.pallas import tpu as pltpu
from jax.sharding import PartitionSpec as P

SP = 5
CALP = 4
CCDS = 62
BSIZE = 128
ITERS = 6
LANES = 128
GROUP = 8
PACKED = 48
attitude_prior = 0.5
f32 = jnp.float32
bf16 = jnp.bfloat16
MESH = pl.DeviceIdType.MESH
VMEM = pltpu.VMEM
nt = (((1,), (1,)), ((), ()))

pairs = [(d, i) for d in range(4) for i in range(4 - d)]


def spline_basis(u):
    rest = 1.0 - u
    square = u * u
    cubed = square * u
    return [
        rest * rest * rest / 6.0,
        (3.0 * cubed - 6.0 * square + 4.0) / 6.0,
        (-3.0 * cubed + 3.0 * square + 3.0 * u + 1.0) / 6.0,
        cubed / 6.0,
    ]


def row_ids():
    return lax.broadcasted_iota(jnp.int32, (8, LANES), 0)


def split_two(x):
    high = x.astype(bf16)
    return high, (x - high.astype(f32)).astype(bf16)


def spread(ref, row, rows=8):
    return jnp.broadcast_to(ref[pl.ds(row, 1), :], (rows, LANES))


def one_hot(index_rows, count):
    ids = lax.broadcasted_iota(jnp.int32, (count, LANES), 0).astype(f32).astype(bf16)
    picked = jnp.broadcast_to(index_rows, (count, LANES)).astype(bf16)
    return jnp.where(picked == ids, jnp.ones((), bf16), jnp.zeros((), bf16))


def fill_owners(counts_ref, owner_ref, owners, blocks, capacity):
    start = jnp.int32(0)
    for o in range(owners):
        for c in range(capacity):
            owner_ref[start + c] = jnp.int32(o)
        start = start + counts_ref[0, o]


def twice(x):
    return jnp.concatenate([x, x], axis=0)


def assemble_kernel(
    owners, capacity, counts_ref, part_ref, phase_ref, weight_ref, resid_ref, offset_ref,
    out_ref, owner_ref, rows_ref, acc_ref,
):
    blocks = phase_ref.shape[0]
    stride = 64
    fill_owners(counts_ref, owner_ref, owners, blocks, capacity)
    acc_ref[...] = jnp.zeros_like(acc_ref)
    rows_ref[...] = jnp.zeros_like(rows_ref)
    low = row_ids() < 4

    def group_step(group, carry):
        base = pl.multiple_of(group * GROUP, GROUP)
        here = pl.ds(base, GROUP)
        spline = spline_basis(phase_ref[here, :])
        weight = weight_ref[here, :]
        weighted = [weight * s for s in spline]
        resid = resid_ref[here, :]

        def put(row, value):
            rows_ref[pl.ds(row, GROUP, stride=stride), :] = value

        for p, (d, i) in enumerate(pairs):
            value = weighted[i] * spline[i + d]
            put(p, value)
            put(16 + 8 * i + 2 * d, value)
            put(16 + 8 * i + 2 * d + 1, value)
        put(10, offset_ref[here, :].astype(f32))
        for i in range(4):
            value = weighted[i] * resid
            for j in range(4):
                put(48 + 4 * i + j, value)
        for q in range(GROUP):
            first = q * stride
            lanes = pl.ds(pl.multiple_of((base + q) * BSIZE, BSIZE), BSIZE)
            a8 = twice(part_ref[0, :, lanes].astype(f32))
            main = a8 * jnp.where(low, a8, pltpu.roll(a8, 7, 0))
            cross = a8 * pltpu.roll(a8, 6, 0)
            features = [main * spread(rows_ref, first + p) for p in range(10)]
            features += [cross * rows_ref[pl.ds(first + 16 + 8 * i, 8), :] for i in range(4)]
            features += [a8 * rows_ref[pl.ds(first + 48 + 8 * h, 8), :] for h in range(2)]
            high, rest = split_two(jnp.concatenate(features, axis=0))
            hot = one_hot(rows_ref[pl.ds(first + 10, 1), :], LANES)
            summed = lax.dot_general(
                jnp.concatenate([high, rest], axis=1), jnp.concatenate([hot, hot], axis=1),
                nt, preferred_element_type=f32,
            )
            owner = owner_ref[base + q]
            acc_ref[owner] = acc_ref[owner] + summed
        return carry

    lax.fori_loop(0, blocks // GROUP, group_step, 0)

    def pack_chip(chip, carry):
        for core in range(2):
            tiles = acc_ref.at[2 * chip + core]

            def shifted(t, i):
                tile = tiles[pl.ds(8 * t, 8), :]
                return tile if i == 0 else pltpu.roll(tile, i, 1)

            for d in range(4):
                total = None
                for p, (pd, i) in enumerate(pairs):
                    if pd == d:
                        term = shifted(p, i)
                        total = term if total is None else total + term
                out_ref[core, chip, pl.ds(8 * d, 8), :] = total
            out_ref[core, chip, pl.ds(32, 8), :] = (
                (shifted(10, 0) + shifted(11, 1)) + (shifted(12, 2) + shifted(13, 3))
            )
            out_ref[core, chip, pl.ds(40, 8), :] = jnp.where(
                low, shifted(14, 0), shifted(14, 1)
            ) + jnp.where(low, shifted(15, 2), shifted(15, 3))
        return carry

    lax.fori_loop(0, owners // 2, pack_chip, 0)


def total_of(x):
    return jnp.sum(jnp.sum(x, axis=1, keepdims=True), axis=0, keepdims=True)


def solve_owner(tiles):
    low = row_ids() < 4
    right_side = tiles[5] + pltpu.roll(tiles[5], 4, 0)
    cross = tiles[4]
    coefficients = []
    for d in range(4):
        first = tiles[d]
        pair_now = cross[2 * d : 2 * d + 2]
        second = jnp.concatenate([pair_now, pair_now, first[7:8], first[4:7]], axis=0)
        if d == 0:
            first = jnp.where(low, first + attitude_prior, first)
            coefficients.append((0, first, second))
            diagonal = jnp.where(low, first, pltpu.roll(first, 4, 0))
        else:
            coefficients.append((d, first, second))
            coefficients.append((-d, pltpu.roll(first, d, 1), pltpu.roll(second, d, 1)))

    def apply_normal(p):
        near = jnp.where(low, p, pltpu.roll(p, 7, 0))
        far = jnp.where(low, pltpu.roll(p, 6, 0), pltpu.roll(p, 5, 0))
        terms = []
        for d, first, second in coefficients:
            if d == 0:
                terms.append(first * near + second * far)
            else:
                shift = (LANES - d) % LANES
                terms.append(first * pltpu.roll(near, shift, 1) + second * pltpu.roll(far, shift, 1))
        result = ((terms[0] + terms[1]) + (terms[2] + terms[3])) + (
            (terms[4] + terms[5]) + terms[6]
        )
        return result + pltpu.roll(result, 4, 0)

    step = jnp.zeros_like(right_side)
    remaining = right_side
    scaled = remaining / diagonal
    direction = scaled
    norm = total_of(remaining * scaled)
    for iteration in range(ITERS):
        image = apply_normal(direction)
        length = norm / total_of(direction * image)
        step = step + length * direction
        if iteration + 1 < ITERS:
            remaining = remaining - length * image
            scaled = remaining / diagonal
            norm_next = total_of(remaining * scaled)
            direction = scaled + norm_next / norm * direction
            norm = norm_next
    return step


def loop(lower, upper, step):
    def run(k, carry):
        step(k)
        return carry

    lax.fori_loop(lower, upper, run, 0)


def refine_kernel(
    owners, segments, owner_ref, parts_ref, part_ref, phase_ref, weight_ref, resid_ref,
    offset_ref, detector_ref, calib_in_ref, source_in_ref, sterm_ref,
    step_ref, calib_ref, source_ref, updated_ref,
    got_pair, mine, got_chip, got_step, rows_ref, table_ref, acc_ref,
    calsum_ref, srcsum_ref, got_cal, got_src,
    pair_send, pair_recv, chip_send, chip_recv, step_send, step_recv,
    cal_send, cal_recv, src_send, src_recv,
):
    chips = owners // 2
    me = lax.axis_index("src")
    segment = lax.axis_index("seg")
    core = lax.rem(me, 2)
    chip = me // 2
    partner = me + 1 - 2 * core
    barrier = pltpu.get_barrier_semaphore()

    def greet_src(k):
        pl.semaphore_signal(
            barrier, inc=1, device_id={"src": lax.rem(me + k, owners)}, device_id_type=MESH
        )

    def greet_seg(k):
        pl.semaphore_signal(
            barrier, inc=1, device_id={"seg": lax.rem(segment + k, segments)}, device_id_type=MESH
        )

    loop(1, owners, greet_src)
    loop(1, segments, greet_seg)
    acc_ref[...] = jnp.zeros_like(acc_ref)
    pl.semaphore_wait(barrier, owners + segments - 2)

    def pair_copy(k):
        target_chip = lax.rem(chip + k, chips)
        return pltpu.make_async_remote_copy(
            src_ref=parts_ref.at[1 - core, target_chip], dst_ref=got_pair.at[k],
            send_sem=pair_send.at[k], recv_sem=pair_recv.at[k],
            device_id={"src": partner}, device_id_type=MESH,
        )

    def chip_copy(k):
        return pltpu.make_async_remote_copy(
            src_ref=mine.at[k], dst_ref=got_chip.at[k],
            send_sem=chip_send.at[k], recv_sem=chip_recv.at[k],
            device_id={"src": 2 * lax.rem(chip + k, chips) + core}, device_id_type=MESH,
        )

    loop(1, chips, lambda k: pair_copy(k).start())
    pair_copy(0).start()

    def add_pair(k):
        pair_copy(k).wait_recv()
        mine[k] = parts_ref[core, lax.rem(chip + k, chips)] + got_pair[k]

    add_pair(1)

    def add_and_send(k):
        add_pair(k)
        chip_copy(k - 1).start()

    loop(2, chips, add_and_send)
    add_pair(0)
    chip_copy(chips - 1).start()

    def gather(k, total):
        chip_copy(k).wait_recv()
        return total + got_chip[k]

    total = lax.fori_loop(1, chips, gather, mine[0])
    step = solve_owner([total[8 * t : 8 * t + 8] for t in range(PACKED // 8)])
    got_step[me] = step[0:4]
    step_ref[0] = step[0:4]

    def step_copy(k, slot):
        return pltpu.make_async_remote_copy(
            src_ref=got_step.at[slot], dst_ref=got_step.at[slot],
            send_sem=step_send.at[k], recv_sem=step_recv.at[slot],
            device_id={"src": lax.rem(me + k, owners)}, device_id_type=MESH,
        )

    loop(1, owners, lambda k: step_copy(k, me).start())

    blocks = phase_ref.shape[0]
    stride = 24
    rows = row_ids()
    low = rows < 4

    def make_table(slot):
        x8 = twice(got_step[slot])
        table = jnp.concatenate(
            [
                jnp.where(low, x8, pltpu.roll(x8, LANES - 1, 1)),
                jnp.where(low, pltpu.roll(x8, LANES - 2, 1), pltpu.roll(x8, LANES - 3, 1)),
            ],
            axis=0,
        )
        high, rest = split_two(table)
        table_ref[slot] = jnp.concatenate([high, rest], axis=0)

    make_table(me)

    def arrive(k):
        slot = lax.rem(me + k, owners)
        step_copy(k, slot).wait_recv()
        make_table(slot)

    loop(1, owners, arrive)

    def group_step(group, carry):
        base = pl.multiple_of(group * GROUP, GROUP)
        here = pl.ds(base, GROUP)
        spline = spline_basis(phase_ref[here, :])

        def put(row, value):
            rows_ref[pl.ds(row, GROUP, stride=stride), :] = value

        put(0, offset_ref[here, :].astype(f32))
        put(1, source_in_ref[here, :].astype(f32))
        put(2, detector_ref[here, :].astype(f32))
        put(3, weight_ref[here, :])
        put(4, resid_ref[here, :])
        for i in range(4):
            for j in range(4):
                put(8 + 4 * i + j, spline[i])
        lefts = []
        rights = []
        for q in range(GROUP):
            first = q * stride
            lanes = pl.ds(pl.multiple_of((base + q) * BSIZE, BSIZE), BSIZE)
            a8 = twice(part_ref[0, :, lanes].astype(f32))
            hot = one_hot(rows_ref[pl.ds(first, 1), :], LANES)
            values = jnp.dot(table_ref[owner_ref[base + q]], hot, preferred_element_type=f32)
            term = a8 * (
                rows_ref[pl.ds(first + 8, 8), :] * (values[0:8] + values[16:24])
                + rows_ref[pl.ds(first + 16, 8), :] * (values[8:16] + values[24:32])
            )
            term = term + pltpu.roll(term, 4, 0)
            term = term + pltpu.roll(term, 2, 0)
            term = term + pltpu.roll(term, 1, 0)
            updated = spread(rows_ref, first + 4) - term
            updated_ref[pl.ds(base + q, 1), :] = updated[0:1]
            weight = spread(rows_ref, first + 3)
            pull = weight * updated
            sterm = sterm_ref[0, :, lanes].astype(f32)
            eight = jnp.concatenate([sterm[0:4], calib_in_ref[0, :, lanes].astype(f32)], axis=0)
            fifth = jnp.broadcast_to(sterm[4:5], (8, LANES))
            last = jnp.where(rows == 0, pull, jnp.where(rows == 1, weight * fifth, 0.0)) * fifth
            high, rest = split_two(
                jnp.concatenate([pull * eight, weight * eight * eight, last], axis=0)
            )
            lefts.append(jnp.concatenate([high.astype(f32), rest.astype(f32)], axis=0).astype(bf16))
            rights.append(
                jnp.concatenate(
                    [
                        one_hot(rows_ref[pl.ds(first + 1, 1), :], LANES),
                        one_hot(rows_ref[pl.ds(first + 2, 1), :], LANES),
                    ],
                    axis=0,
                )
            )
        acc_ref[...] += lax.dot_general(
            jnp.concatenate(lefts, axis=1), jnp.concatenate(rights, axis=1), nt,
            preferred_element_type=f32,
        )
        return carry

    lax.fori_loop(0, blocks // GROUP, group_step, 0)
    sums = acc_ref[0:24] + acc_ref[24:48]
    for_source = sums[:, 0:LANES]
    for_calib = sums[:, LANES : 2 * LANES]
    srcsum_ref[0:8] = jnp.concatenate([for_source[0:4], for_source[8:12]], axis=0)
    srcsum_ref[8:16] = for_source[16:24]
    lane = lax.broadcasted_iota(jnp.int32, (4, LANES), 1)
    calsum_ref[...] = jnp.where(lane < 64, for_calib[4:8], pltpu.roll(for_calib, 64, 1)[12:16])

    def src_copy(k, slot):
        return pltpu.make_async_remote_copy(
            src_ref=srcsum_ref, dst_ref=got_src.at[slot],
            send_sem=src_send.at[k], recv_sem=src_recv.at[slot],
            device_id={"seg": lax.rem(segment + k, segments)}, device_id_type=MESH,
        )

    def cal_copy(k, slot):
        return pltpu.make_async_remote_copy(
            src_ref=calsum_ref, dst_ref=got_cal.at[slot],
            send_sem=cal_send.at[k], recv_sem=cal_recv.at[slot],
            device_id={"src": lax.rem(me + k, owners)}, device_id_type=MESH,
        )

    got_src[segment] = srcsum_ref[...]
    got_cal[me] = calsum_ref[...]
    loop(1, segments, lambda k: src_copy(k, segment).start())
    loop(1, owners, lambda k: cal_copy(k, me).start())

    def drain(k):
        pair_copy(k).wait_send()
        chip_copy(k).wait_send()

    loop(1, chips, drain)
    pair_copy(0).wait_send()
    loop(1, owners, lambda k: step_copy(k, me).wait_send())
    loop(1, segments, lambda k: src_copy(k, lax.rem(segment + k, segments)).wait_recv())
    total = got_src[0]
    for k in range(1, segments):
        total = total + got_src[k]
    source_ref[0:4] = total[0:4] / (1.0 + total[4:8])
    source_ref[4:5] = total[8:9] / (1.0 + total[9:10])
    loop(1, owners, lambda k: cal_copy(k, lax.rem(me + k, owners)).wait_recv())
    total = got_cal[0]
    for k in range(1, owners):
        total = total + got_cal[k]
    result = total / (1.0 + pltpu.roll(total, 64, 1))
    calib_ref[0] = result[:, 0:CCDS]
    loop(1, segments, lambda k: src_copy(k, segment).wait_send())
    loop(1, owners, lambda k: cal_copy(k, me).wait_send())


def body(
    attitude_partials, scan_phase, huber_weight, residual, knot_offset, detector_index,
    calibration_partials, source_index, source_partials, send_counts,
):
    owners = lax.axis_size("src")
    segments = lax.axis_size("seg")
    blocks = scan_phase.shape[1] // BSIZE
    capacity = 2 * blocks // owners
    chips = owners // 2
    spec = pl.BlockSpec(memory_space=VMEM)
    scalars = pl.BlockSpec(memory_space=pltpu.SMEM)
    shape = jax.ShapeDtypeStruct
    dma = pltpu.SemaphoreType.DMA

    def by_block(x):
        return x.reshape(blocks, BSIZE)

    phase, weight, resid, offset = map(by_block, (scan_phase, huber_weight, residual, knot_offset))
    parts, owner_of = pl.pallas_call(
        functools.partial(assemble_kernel, owners, capacity),
        out_shape=(shape((2, chips, PACKED, LANES), f32), shape((blocks + capacity,), jnp.int32)),
        in_specs=[scalars] + [spec] * 5,
        out_specs=(spec, scalars),
        scratch_shapes=[VMEM((GROUP * 64, LANES), f32), VMEM((owners, LANES, LANES), f32)],
        name="assemble",
    )(send_counts.reshape(1, owners), attitude_partials, phase, weight, resid, offset)
    step, calib, source, updated = pl.pallas_call(
        functools.partial(refine_kernel, owners, segments),
        out_shape=(
            shape((1, 4, LANES), f32), shape((1, CALP, CCDS), f32), shape((SP, LANES), f32),
            shape((blocks, BSIZE), f32),
        ),
        in_specs=[scalars] + [spec] * 10,
        out_specs=(spec,) * 4,
        scratch_shapes=[VMEM((chips, PACKED, LANES), f32)] * 3
        + [
            VMEM((owners, 4, LANES), f32), VMEM((GROUP * 24, LANES), f32),
            VMEM((owners, 32, LANES), bf16), VMEM((48, 2 * LANES), f32),
            VMEM((4, LANES), f32), VMEM((16, LANES), f32),
            VMEM((owners, 4, LANES), f32), VMEM((segments, 16, LANES), f32),
        ]
        + [dma((chips,))] * 4
        + [dma((owners,))] * 4
        + [dma((segments,))] * 2,
        compiler_params=pltpu.CompilerParams(collective_id=0, has_side_effects=True),
        name="refine",
    )(
        owner_of, parts, attitude_partials, phase, weight, resid, offset,
        by_block(detector_index), calibration_partials, by_block(source_index), source_partials,
    )
    return (step, calib, source, updated.reshape(1, blocks * BSIZE))


def solution(mesh):
    return jax.shard_map(
        body,
        mesh=mesh,
        in_specs=(
            P("seg", None, "src"),
            P("seg", "src"),
            P("seg", "src"),
            P("seg", "src"),
            P("seg", "src"),
            P("seg", "src"),
            P("seg", None, "src"),
            P("seg", "src"),
            P("seg", None, "src"),
            P("seg", "src", None),
        ),
        out_specs=(P("seg", None, "src"), P("seg", None, None), P(None, "src"), P("seg", "src")),
        check_vma=False,
    )
```

```python
import functools

import jax
import jax.numpy as jnp
from jax import lax
from jax.experimental import pallas as pl
from jax.experimental.pallas import tpu as pltpu
from jax.sharding import PartitionSpec as P

SP = 5
CALP = 4
CCDS = 62
BSIZE = 128
ITERS = 6
LANES = 128
GROUP = 8
PACKED = 48
attitude_prior = 0.5
f32 = jnp.float32
bf16 = jnp.bfloat16
MESH = pl.DeviceIdType.MESH
VMEM = pltpu.VMEM
nt = (((1,), (1,)), ((), ()))

pairs = [(d, i) for d in range(4) for i in range(4 - d)]


def spline_basis(u):
    rest = 1.0 - u
    square = u * u
    cubed = square * u
    return [
        rest * rest * rest / 6.0,
        (3.0 * cubed - 6.0 * square + 4.0) / 6.0,
        (-3.0 * cubed + 3.0 * square + 3.0 * u + 1.0) / 6.0,
        cubed / 6.0,
    ]


def row_ids():
    return lax.broadcasted_iota(jnp.int32, (8, LANES), 0)


def split_two(x):
    high = x.astype(bf16)
    return high, (x - high.astype(f32)).astype(bf16)


def spread(ref, row, rows=8):
    return jnp.broadcast_to(ref[pl.ds(row, 1), :], (rows, LANES))


def one_hot(index_rows, count):
    ids = lax.broadcasted_iota(jnp.int32, (count, LANES), 0).astype(f32).astype(bf16)
    picked = jnp.broadcast_to(index_rows, (count, LANES)).astype(bf16)
    return jnp.where(picked == ids, jnp.ones((), bf16), jnp.zeros((), bf16))


def fill_owners(counts_ref, owner_ref, owners, blocks, capacity):
    start = jnp.int32(0)
    for o in range(owners):
        for c in range(capacity):
            owner_ref[start + c] = jnp.int32(o)
        start = start + counts_ref[0, o]


def twice(x):
    return jnp.concatenate([x, x], axis=0)


def assemble_kernel(
    owners, capacity, counts_ref, part_ref, phase_ref, weight_ref, resid_ref, offset_ref,
    out_ref, owner_ref, rows_ref, acc_ref,
):
    blocks = phase_ref.shape[0]
    stride = 64
    fill_owners(counts_ref, owner_ref, owners, blocks, capacity)
    acc_ref[...] = jnp.zeros_like(acc_ref)
    rows_ref[...] = jnp.zeros_like(rows_ref)
    low = row_ids() < 4

    def group_step(group, carry):
        base = pl.multiple_of(group * GROUP, GROUP)
        here = pl.ds(base, GROUP)
        spline = spline_basis(phase_ref[here, :])
        weight = weight_ref[here, :]
        weighted = [weight * s for s in spline]
        resid = resid_ref[here, :]

        def put(row, value):
            rows_ref[pl.ds(row, GROUP, stride=stride), :] = value

        for p, (d, i) in enumerate(pairs):
            value = weighted[i] * spline[i + d]
            put(p, value)
            put(16 + 8 * i + 2 * d, value)
            put(16 + 8 * i + 2 * d + 1, value)
        put(10, offset_ref[here, :].astype(f32))
        for i in range(4):
            value = weighted[i] * resid
            for j in range(4):
                put(48 + 4 * i + j, value)
        for q in range(GROUP):
            first = q * stride
            lanes = pl.ds(pl.multiple_of((base + q) * BSIZE, BSIZE), BSIZE)
            a8 = twice(part_ref[0, :, lanes].astype(f32))
            main = a8 * jnp.where(low, a8, pltpu.roll(a8, 7, 0))
            cross = a8 * pltpu.roll(a8, 6, 0)
            features = [main * spread(rows_ref, first + p) for p in range(10)]
            features += [cross * rows_ref[pl.ds(first + 16 + 8 * i, 8), :] for i in range(4)]
            features += [a8 * rows_ref[pl.ds(first + 48 + 8 * h, 8), :] for h in range(2)]
            high, rest = split_two(jnp.concatenate(features, axis=0))
            hot = one_hot(rows_ref[pl.ds(first + 10, 1), :], LANES)
            summed = lax.dot_general(
                jnp.concatenate([high, rest], axis=1), jnp.concatenate([hot, hot], axis=1),
                nt, preferred_element_type=f32,
            )
            owner = owner_ref[base + q]
            acc_ref[owner] = acc_ref[owner] + summed
        return carry

    lax.fori_loop(0, blocks // GROUP, group_step, 0)

    def pack_chip(chip, carry):
        for core in range(2):
            tiles = acc_ref.at[2 * chip + core]

            def shifted(t, i):
                tile = tiles[pl.ds(8 * t, 8), :]
                return tile if i == 0 else pltpu.roll(tile, i, 1)

            for d in range(4):
                total = None
                for p, (pd, i) in enumerate(pairs):
                    if pd == d:
                        term = shifted(p, i)
                        total = term if total is None else total + term
                out_ref[core, chip, pl.ds(8 * d, 8), :] = total
            out_ref[core, chip, pl.ds(32, 8), :] = (
                (shifted(10, 0) + shifted(11, 1)) + (shifted(12, 2) + shifted(13, 3))
            )
            out_ref[core, chip, pl.ds(40, 8), :] = jnp.where(
                low, shifted(14, 0), shifted(14, 1)
            ) + jnp.where(low, shifted(15, 2), shifted(15, 3))
        return carry

    lax.fori_loop(0, owners // 2, pack_chip, 0)


def total_of(x):
    return jnp.sum(jnp.sum(x, axis=1, keepdims=True), axis=0, keepdims=True)


def solve_owner(tiles):
    low = row_ids() < 4
    right_side = tiles[5] + pltpu.roll(tiles[5], 4, 0)
    cross = tiles[4]
    coefficients = []
    for d in range(4):
        first = tiles[d]
        pair_now = cross[2 * d : 2 * d + 2]
        second = jnp.concatenate([pair_now, pair_now, first[7:8], first[4:7]], axis=0)
        if d == 0:
            first = jnp.where(low, first + attitude_prior, first)
            coefficients.append((0, first, second))
            diagonal = jnp.where(low, first, pltpu.roll(first, 4, 0))
        else:
            coefficients.append((d, first, second))
            coefficients.append((-d, pltpu.roll(first, d, 1), pltpu.roll(second, d, 1)))

    def apply_normal(p):
        near = jnp.where(low, p, pltpu.roll(p, 7, 0))
        far = jnp.where(low, pltpu.roll(p, 6, 0), pltpu.roll(p, 5, 0))
        terms = []
        for d, first, second in coefficients:
            if d == 0:
                terms.append(first * near + second * far)
            else:
                shift = (LANES - d) % LANES
                terms.append(first * pltpu.roll(near, shift, 1) + second * pltpu.roll(far, shift, 1))
        result = ((terms[0] + terms[1]) + (terms[2] + terms[3])) + (
            (terms[4] + terms[5]) + terms[6]
        )
        return result + pltpu.roll(result, 4, 0)

    step = jnp.zeros_like(right_side)
    remaining = right_side
    scaled = remaining / diagonal
    direction = scaled
    norm = total_of(remaining * scaled)
    for iteration in range(ITERS):
        image = apply_normal(direction)
        length = norm / total_of(direction * image)
        step = step + length * direction
        if iteration + 1 < ITERS:
            remaining = remaining - length * image
            scaled = remaining / diagonal
            norm_next = total_of(remaining * scaled)
            direction = scaled + norm_next / norm * direction
            norm = norm_next
    return step


def loop(lower, upper, step):
    def run(k, carry):
        step(k)
        return carry

    lax.fori_loop(lower, upper, run, 0)


def refine_kernel(
    owners, segments, owner_ref, parts_ref, part_ref, phase_ref, weight_ref, resid_ref,
    offset_ref, detector_ref, calib_in_ref, source_in_ref, sterm_ref,
    step_ref, calib_ref, source_ref, updated_ref,
    got_pair, mine, got_chip, got_step, rows_ref, table_ref, pull_acc, damp_acc,
    hot_ref, right_ref, design_ref, scaled_ref,
    calsum_ref, srcsum_ref, got_cal, got_src,
    pair_send, pair_recv, chip_send, chip_recv, step_send, step_recv,
    cal_send, cal_recv, src_send, src_recv,
):
    chips = owners // 2
    me = lax.axis_index("src")
    segment = lax.axis_index("seg")
    core = lax.rem(me, 2)
    chip = me // 2
    partner = me + 1 - 2 * core
    barrier = pltpu.get_barrier_semaphore()

    def greet_src(k):
        pl.semaphore_signal(
            barrier, inc=1, device_id={"src": lax.rem(me + k, owners)}, device_id_type=MESH
        )

    def greet_seg(k):
        pl.semaphore_signal(
            barrier, inc=1, device_id={"seg": lax.rem(segment + k, segments)}, device_id_type=MESH
        )

    loop(1, owners, greet_src)
    loop(1, segments, greet_seg)
    blocks = phase_ref.shape[0]
    groups = blocks // GROUP
    stride = 24
    rows = row_ids()
    low = rows < 4
    pull_acc[...] = jnp.zeros_like(pull_acc)
    damp_acc[...] = jnp.zeros_like(damp_acc)

    def prepare(group):
        base = pl.multiple_of(group * GROUP, GROUP)
        here = pl.ds(base, GROUP)
        spline = spline_basis(phase_ref[here, :])

        def put(row, value):
            rows_ref[pl.ds(row, GROUP, stride=stride), :] = value

        put(0, offset_ref[here, :].astype(f32))
        put(1, source_in_ref[here, :].astype(f32))
        put(2, detector_ref[here, :].astype(f32))
        put(3, weight_ref[here, :])
        for i in range(4):
            for j in range(4):
                put(8 + 4 * i + j, spline[i])
        lefts = []
        for q in range(GROUP):
            first = q * stride
            lanes = pl.ds(pl.multiple_of((base + q) * BSIZE, BSIZE), BSIZE)
            here_lanes = slice(q * BSIZE, (q + 1) * BSIZE)
            a8 = twice(part_ref[0, :, lanes].astype(f32))
            design_ref[base + q, 0:8] = a8 * rows_ref[pl.ds(first + 8, 8), :]
            design_ref[base + q, 8:16] = a8 * rows_ref[pl.ds(first + 16, 8), :]
            hot_ref[base + q] = one_hot(rows_ref[pl.ds(first, 1), :], LANES)
            right_ref[group, 0:LANES, here_lanes] = one_hot(rows_ref[pl.ds(first + 1, 1), :], LANES)
            right_ref[group, LANES:, here_lanes] = one_hot(rows_ref[pl.ds(first + 2, 1), :], LANES)
            weight = spread(rows_ref, first + 3)
            sterm = sterm_ref[0, :, lanes].astype(f32)
            eight = jnp.concatenate([sterm[0:4], calib_in_ref[0, :, lanes].astype(f32)], axis=0)
            fifth = jnp.broadcast_to(sterm[4:5], (8, LANES))
            scaled = weight * eight
            scaled_fifth = jnp.where(rows == 0, weight * fifth, 0.0)
            scaled_ref[base + q, 0:8] = scaled
            scaled_ref[base + q, 8:16] = scaled_fifth
            high, rest = split_two(jnp.concatenate([scaled * eight, scaled_fifth * fifth], axis=0))
            lefts.append(jnp.concatenate([high, rest], axis=0))
        damp_acc[...] += lax.dot_general(
            jnp.concatenate(lefts, axis=1), right_ref[group], nt, preferred_element_type=f32
        )

    early = groups // 4
    middle = 3 * groups // 4
    loop(0, early, prepare)
    pl.semaphore_wait(barrier, owners + segments - 2)

    def pair_copy(k):
        target_chip = lax.rem(chip + k, chips)
        return pltpu.make_async_remote_copy(
            src_ref=parts_ref.at[1 - core, target_chip], dst_ref=got_pair.at[k],
            send_sem=pair_send.at[k], recv_sem=pair_recv.at[k],
            device_id={"src": partner}, device_id_type=MESH,
        )

    def chip_copy(k):
        return pltpu.make_async_remote_copy(
            src_ref=mine.at[k], dst_ref=got_chip.at[k],
            send_sem=chip_send.at[k], recv_sem=chip_recv.at[k],
            device_id={"src": 2 * lax.rem(chip + k, chips) + core}, device_id_type=MESH,
        )

    loop(1, chips, lambda k: pair_copy(k).start())
    pair_copy(0).start()

    def add_pair(k):
        pair_copy(k).wait_recv()
        mine[k] = parts_ref[core, lax.rem(chip + k, chips)] + got_pair[k]

    add_pair(1)

    def add_and_send(k):
        add_pair(k)
        chip_copy(k - 1).start()

    loop(2, chips, add_and_send)
    add_pair(0)
    chip_copy(chips - 1).start()
    loop(early, middle, prepare)

    def gather(k, total):
        chip_copy(k).wait_recv()
        return total + got_chip[k]

    total = lax.fori_loop(1, chips, gather, mine[0])
    step = solve_owner([total[8 * t : 8 * t + 8] for t in range(PACKED // 8)])
    got_step[me] = step[0:4]
    step_ref[0] = step[0:4]

    def step_copy(k, slot):
        return pltpu.make_async_remote_copy(
            src_ref=got_step.at[slot], dst_ref=got_step.at[slot],
            send_sem=step_send.at[k], recv_sem=step_recv.at[slot],
            device_id={"src": lax.rem(me + k, owners)}, device_id_type=MESH,
        )

    loop(1, owners, lambda k: step_copy(k, me).start())
    loop(middle, groups, prepare)

    def make_table(slot):
        x8 = twice(got_step[slot])
        table = jnp.concatenate(
            [
                jnp.where(low, x8, pltpu.roll(x8, LANES - 1, 1)),
                jnp.where(low, pltpu.roll(x8, LANES - 2, 1), pltpu.roll(x8, LANES - 3, 1)),
            ],
            axis=0,
        )
        high, rest = split_two(table)
        table_ref[slot] = jnp.concatenate([high, rest], axis=0)

    make_table(me)

    def arrive(k):
        slot = lax.rem(me + k, owners)
        step_copy(k, slot).wait_recv()
        make_table(slot)

    loop(1, owners, arrive)

    def correct(group):
        base = pl.multiple_of(group * GROUP, GROUP)
        lefts = []
        for q in range(GROUP):
            block = base + q
            values = jnp.dot(
                table_ref[owner_ref[block]], hot_ref[block], preferred_element_type=f32
            )
            term = design_ref[block, 0:8] * (values[0:8] + values[16:24]) + design_ref[
                block, 8:16
            ] * (values[8:16] + values[24:32])
            term = term + pltpu.roll(term, 4, 0)
            term = term + pltpu.roll(term, 2, 0)
            term = term + pltpu.roll(term, 1, 0)
            updated = spread(resid_ref, block) - term
            updated_ref[pl.ds(block, 1), :] = updated[0:1]
            high, rest = split_two(
                jnp.concatenate(
                    [updated * scaled_ref[block, 0:8], updated * scaled_ref[block, 8:16]], axis=0
                )
            )
            lefts.append(jnp.concatenate([high, rest], axis=0))
        pull_acc[...] += lax.dot_general(
            jnp.concatenate(lefts, axis=1), right_ref[group], nt, preferred_element_type=f32
        )

    loop(0, groups, correct)
    pull = pull_acc[0:16] + pull_acc[16:32]
    damp = damp_acc[0:16] + damp_acc[16:32]
    srcsum_ref[0:8] = jnp.concatenate([pull[0:4, 0:LANES], damp[0:4, 0:LANES]], axis=0)
    srcsum_ref[8:16] = pull[8:16, 0:LANES] + pltpu.roll(damp[8:16, 0:LANES], 1, 0)
    lane = lax.broadcasted_iota(jnp.int32, (8, LANES), 1)
    both = jnp.where(lane < 64, pull[0:8, LANES:], pltpu.roll(damp[0:8, LANES:], 64, 1))
    calsum_ref[...] = both[4:8]

    def src_copy(k, slot):
        return pltpu.make_async_remote_copy(
            src_ref=srcsum_ref, dst_ref=got_src.at[slot],
            send_sem=src_send.at[k], recv_sem=src_recv.at[slot],
            device_id={"seg": lax.rem(segment + k, segments)}, device_id_type=MESH,
        )

    def cal_copy(k, slot):
        return pltpu.make_async_remote_copy(
            src_ref=calsum_ref, dst_ref=got_cal.at[slot],
            send_sem=cal_send.at[k], recv_sem=cal_recv.at[slot],
            device_id={"src": lax.rem(me + k, owners)}, device_id_type=MESH,
        )

    got_src[segment] = srcsum_ref[...]
    got_cal[me] = calsum_ref[...]
    loop(1, segments, lambda k: src_copy(k, segment).start())
    loop(1, owners, lambda k: cal_copy(k, me).start())

    def drain(k):
        pair_copy(k).wait_send()
        chip_copy(k).wait_send()

    loop(1, chips, drain)
    pair_copy(0).wait_send()
    loop(1, owners, lambda k: step_copy(k, me).wait_send())
    loop(1, segments, lambda k: src_copy(k, lax.rem(segment + k, segments)).wait_recv())
    total = got_src[0]
    for k in range(1, segments):
        total = total + got_src[k]
    source_ref[0:4] = total[0:4] / (1.0 + total[4:8])
    source_ref[4:5] = total[8:9] / (1.0 + total[9:10])
    loop(1, owners, lambda k: cal_copy(k, lax.rem(me + k, owners)).wait_recv())
    total = got_cal[0]
    for k in range(1, owners):
        total = total + got_cal[k]
    result = total / (1.0 + pltpu.roll(total, 64, 1))
    calib_ref[0] = result[:, 0:CCDS]
    loop(1, segments, lambda k: src_copy(k, segment).wait_send())
    loop(1, owners, lambda k: cal_copy(k, me).wait_send())


def hand_out_kernel(*refs):
    for given, out in zip(refs[:4], refs[4:]):
        out[...] = given[...]


def body(
    attitude_partials, scan_phase, huber_weight, residual, knot_offset, detector_index,
    calibration_partials, source_index, source_partials, send_counts,
):
    owners = lax.axis_size("src")
    segments = lax.axis_size("seg")
    blocks = scan_phase.shape[1] // BSIZE
    capacity = 2 * blocks // owners
    chips = owners // 2
    spec = pl.BlockSpec(memory_space=VMEM)
    scalars = pl.BlockSpec(memory_space=pltpu.SMEM)
    shape = jax.ShapeDtypeStruct
    dma = pltpu.SemaphoreType.DMA

    def by_block(x):
        return x.reshape(blocks, BSIZE)

    phase, weight, resid, offset = map(by_block, (scan_phase, huber_weight, residual, knot_offset))
    parts, owner_of = pl.pallas_call(
        functools.partial(assemble_kernel, owners, capacity),
        out_shape=(shape((2, chips, PACKED, LANES), f32), shape((blocks + capacity,), jnp.int32)),
        in_specs=[scalars] + [spec] * 5,
        out_specs=(spec, scalars),
        scratch_shapes=[VMEM((GROUP * 64, LANES), f32), VMEM((owners, LANES, LANES), f32)],
        name="assemble",
    )(send_counts.reshape(1, owners), attitude_partials, phase, weight, resid, offset)
    results = (
        shape((1, 4, LANES), f32), shape((1, CALP, CCDS), f32), shape((SP, LANES), f32),
        shape((blocks, BSIZE), f32),
    )
    refined = pl.pallas_call(
        functools.partial(refine_kernel, owners, segments),
        out_shape=results,
        in_specs=[scalars] + [spec] * 10,
        out_specs=(spec,) * 4,
        scratch_shapes=[VMEM((chips, PACKED, LANES), f32)] * 3
        + [
            VMEM((owners, 4, LANES), f32), VMEM((GROUP * 24, LANES), f32),
            VMEM((owners, 32, LANES), bf16), VMEM((32, 2 * LANES), f32),
            VMEM((32, 2 * LANES), f32), VMEM((blocks, LANES, BSIZE), bf16),
            VMEM((blocks // GROUP, 2 * LANES, GROUP * BSIZE), bf16),
            VMEM((blocks, 16, BSIZE), f32), VMEM((blocks, 16, BSIZE), f32),
            VMEM((4, LANES), f32), VMEM((16, LANES), f32),
            VMEM((owners, 4, LANES), f32), VMEM((segments, 16, LANES), f32),
        ]
        + [dma((chips,))] * 4
        + [dma((owners,))] * 4
        + [dma((segments,))] * 2,
        compiler_params=pltpu.CompilerParams(
            collective_id=0, has_side_effects=True, vmem_limit_bytes=67043328
        ),
        name="refine",
    )(
        owner_of, parts, attitude_partials, phase, weight, resid, offset,
        by_block(detector_index), calibration_partials, by_block(source_index), source_partials,
    )
    step, calib, source, updated = pl.pallas_call(
        hand_out_kernel,
        out_shape=results,
        in_specs=[spec] * 4,
        out_specs=(spec,) * 4,
        name="hand_out",
    )(*refined)
    return (step, calib, source, updated.reshape(1, blocks * BSIZE))


def solution(mesh):
    return jax.shard_map(
        body,
        mesh=mesh,
        in_specs=(
            P("seg", None, "src"),
            P("seg", "src"),
            P("seg", "src"),
            P("seg", "src"),
            P("seg", "src"),
            P("seg", "src"),
            P("seg", None, "src"),
            P("seg", "src"),
            P("seg", None, "src"),
            P("seg", "src", None),
        ),
        out_specs=(P("seg", None, "src"), P("seg", None, None), P(None, "src"), P("seg", "src")),
        check_vma=False,
    )
```

```python
import functools

import jax
import jax.numpy as jnp
from jax import lax
from jax.experimental import pallas as pl
from jax.experimental.pallas import tpu as pltpu
from jax.sharding import PartitionSpec as P

SP = 5
CALP = 4
CCDS = 62
BSIZE = 128
ITERS = 6
LANES = 128
GROUP = 8
PACKED = 48
attitude_prior = 0.5
f32 = jnp.float32
bf16 = jnp.bfloat16
MESH = pl.DeviceIdType.MESH
VMEM = pltpu.VMEM
nt = (((1,), (1,)), ((), ()))

pairs = [(d, i) for d in range(4) for i in range(4 - d)]


def spline_basis(u):
    rest = 1.0 - u
    square = u * u
    cubed = square * u
    return [
        rest * rest * rest / 6.0,
        (3.0 * cubed - 6.0 * square + 4.0) / 6.0,
        (-3.0 * cubed + 3.0 * square + 3.0 * u + 1.0) / 6.0,
        cubed / 6.0,
    ]


def row_ids():
    return lax.broadcasted_iota(jnp.int32, (8, LANES), 0)


def split_two(x):
    high = x.astype(bf16)
    return high, (x - high.astype(f32)).astype(bf16)


def spread(ref, row, rows=8):
    return jnp.broadcast_to(ref[pl.ds(row, 1), :], (rows, LANES))


def one_hot(index_rows, count):
    ids = lax.broadcasted_iota(jnp.int32, (count, LANES), 0).astype(f32).astype(bf16)
    picked = jnp.broadcast_to(index_rows, (count, LANES)).astype(bf16)
    return jnp.where(picked == ids, jnp.ones((), bf16), jnp.zeros((), bf16))


def fill_owners(counts_ref, owner_ref, owners, blocks, capacity):
    start = jnp.int32(0)
    for o in range(owners):
        for c in range(capacity):
            owner_ref[start + c] = jnp.int32(o)
        start = start + counts_ref[0, o]


def twice(x):
    return jnp.concatenate([x, x], axis=0)


def assemble_kernel(
    owners, capacity, counts_ref, part_ref, phase_ref, weight_ref, resid_ref, offset_ref,
    out_ref, owner_ref, rows_ref, acc_ref,
):
    blocks = phase_ref.shape[0]
    stride = 64
    fill_owners(counts_ref, owner_ref, owners, blocks, capacity)
    acc_ref[...] = jnp.zeros_like(acc_ref)
    rows_ref[...] = jnp.zeros_like(rows_ref)
    low = row_ids() < 4

    def group_step(group, carry):
        base = pl.multiple_of(group * GROUP, GROUP)
        here = pl.ds(base, GROUP)
        spline = spline_basis(phase_ref[here, :])
        weight = weight_ref[here, :]
        weighted = [weight * s for s in spline]
        resid = resid_ref[here, :]

        def put(row, value):
            rows_ref[pl.ds(row, GROUP, stride=stride), :] = value

        for p, (d, i) in enumerate(pairs):
            value = weighted[i] * spline[i + d]
            put(p, value)
            put(16 + 8 * i + 2 * d, value)
            put(16 + 8 * i + 2 * d + 1, value)
        put(10, offset_ref[here, :].astype(f32))
        for i in range(4):
            value = weighted[i] * resid
            for j in range(4):
                put(48 + 4 * i + j, value)
        for q in range(GROUP):
            first = q * stride
            lanes = pl.ds(pl.multiple_of((base + q) * BSIZE, BSIZE), BSIZE)
            a8 = twice(part_ref[0, :, lanes].astype(f32))
            main = a8 * jnp.where(low, a8, pltpu.roll(a8, 7, 0))
            cross = a8 * pltpu.roll(a8, 6, 0)
            features = [main * spread(rows_ref, first + p) for p in range(10)]
            features += [cross * rows_ref[pl.ds(first + 16 + 8 * i, 8), :] for i in range(4)]
            features += [a8 * rows_ref[pl.ds(first + 48 + 8 * h, 8), :] for h in range(2)]
            high, rest = split_two(jnp.concatenate(features, axis=0))
            hot = one_hot(rows_ref[pl.ds(first + 10, 1), :], LANES)
            summed = lax.dot_general(
                jnp.concatenate([high, rest], axis=1), jnp.concatenate([hot, hot], axis=1),
                nt, preferred_element_type=f32,
            )
            owner = owner_ref[base + q]
            acc_ref[owner] = acc_ref[owner] + summed
        return carry

    lax.fori_loop(0, blocks // GROUP, group_step, 0)

    def pack_chip(chip, carry):
        for core in range(2):
            tiles = acc_ref.at[2 * chip + core]

            def shifted(t, i):
                tile = tiles[pl.ds(8 * t, 8), :]
                return tile if i == 0 else pltpu.roll(tile, i, 1)

            for d in range(4):
                total = None
                for p, (pd, i) in enumerate(pairs):
                    if pd == d:
                        term = shifted(p, i)
                        total = term if total is None else total + term
                out_ref[core, chip, pl.ds(8 * d, 8), :] = total
            out_ref[core, chip, pl.ds(32, 8), :] = (
                (shifted(10, 0) + shifted(11, 1)) + (shifted(12, 2) + shifted(13, 3))
            )
            out_ref[core, chip, pl.ds(40, 8), :] = jnp.where(
                low, shifted(14, 0), shifted(14, 1)
            ) + jnp.where(low, shifted(15, 2), shifted(15, 3))
        return carry

    lax.fori_loop(0, owners // 2, pack_chip, 0)


def total_of(x):
    return jnp.sum(jnp.sum(x, axis=1, keepdims=True), axis=0, keepdims=True)


def solve_owner(tiles):
    low = row_ids() < 4
    right_side = tiles[5] + pltpu.roll(tiles[5], 4, 0)
    cross = tiles[4]
    coefficients = []
    for d in range(4):
        first = tiles[d]
        pair_now = cross[2 * d : 2 * d + 2]
        second = jnp.concatenate([pair_now, pair_now, first[7:8], first[4:7]], axis=0)
        if d == 0:
            first = jnp.where(low, first + attitude_prior, first)
            coefficients.append((0, first, second))
            diagonal = jnp.where(low, first, pltpu.roll(first, 4, 0))
        else:
            coefficients.append((d, first, second))
            coefficients.append((-d, pltpu.roll(first, d, 1), pltpu.roll(second, d, 1)))

    def apply_normal(p):
        near = jnp.where(low, p, pltpu.roll(p, 7, 0))
        far = jnp.where(low, pltpu.roll(p, 6, 0), pltpu.roll(p, 5, 0))
        terms = []
        for d, first, second in coefficients:
            if d == 0:
                terms.append(first * near + second * far)
            else:
                shift = (LANES - d) % LANES
                terms.append(first * pltpu.roll(near, shift, 1) + second * pltpu.roll(far, shift, 1))
        result = ((terms[0] + terms[1]) + (terms[2] + terms[3])) + (
            (terms[4] + terms[5]) + terms[6]
        )
        return result + pltpu.roll(result, 4, 0)

    step = jnp.zeros_like(right_side)
    remaining = right_side
    scaled = remaining / diagonal
    direction = scaled
    norm = total_of(remaining * scaled)
    for iteration in range(ITERS):
        image = apply_normal(direction)
        length = norm / total_of(direction * image)
        step = step + length * direction
        if iteration + 1 < ITERS:
            remaining = remaining - length * image
            scaled = remaining / diagonal
            norm_next = total_of(remaining * scaled)
            direction = scaled + norm_next / norm * direction
            norm = norm_next
    return step


def loop(lower, upper, step):
    def run(k, carry):
        step(k)
        return carry

    lax.fori_loop(lower, upper, run, 0)


def refine_kernel(
    owners, segments, owner_ref, parts_ref, part_ref, phase_ref, weight_ref, resid_ref,
    offset_ref, detector_ref, calib_in_ref, source_in_ref, sterm_ref,
    step_ref, calib_ref, source_ref, updated_ref,
    got_pair, mine, got_chip, got_step, rows_ref, table_ref, pull_acc, damp_acc,
    hot_ref, right_ref, design_ref, scaled_ref,
    calsum_ref, srcsum_ref, got_cal, got_src,
    pair_send, pair_recv, chip_send, chip_recv, step_send, step_recv,
    cal_send, cal_recv, src_send, src_recv,
):
    chips = owners // 2
    me = lax.axis_index("src")
    segment = lax.axis_index("seg")
    core = lax.rem(me, 2)
    chip = me // 2
    partner = me + 1 - 2 * core
    barrier = pltpu.get_barrier_semaphore()

    def greet_src(k):
        pl.semaphore_signal(
            barrier, inc=1, device_id={"src": lax.rem(me + k, owners)}, device_id_type=MESH
        )

    def greet_seg(k):
        pl.semaphore_signal(
            barrier, inc=1, device_id={"seg": lax.rem(segment + k, segments)}, device_id_type=MESH
        )

    loop(1, owners, greet_src)
    loop(1, segments, greet_seg)
    blocks = phase_ref.shape[0]
    groups = blocks // GROUP
    stride = 24
    rows = row_ids()
    low = rows < 4
    pull_acc[...] = jnp.zeros_like(pull_acc)
    damp_acc[...] = jnp.zeros_like(damp_acc)

    def prepare(group):
        base = pl.multiple_of(group * GROUP, GROUP)
        here = pl.ds(base, GROUP)
        spline = spline_basis(phase_ref[here, :])

        def put(row, value):
            rows_ref[pl.ds(row, GROUP, stride=stride), :] = value

        put(0, offset_ref[here, :].astype(f32))
        put(1, source_in_ref[here, :].astype(f32))
        put(2, detector_ref[here, :].astype(f32))
        put(3, weight_ref[here, :])
        for i in range(4):
            for j in range(4):
                put(8 + 4 * i + j, spline[i])
        lefts = []
        for q in range(GROUP):
            first = q * stride
            lanes = pl.ds(pl.multiple_of((base + q) * BSIZE, BSIZE), BSIZE)
            here_lanes = slice(q * BSIZE, (q + 1) * BSIZE)
            a8 = twice(part_ref[0, :, lanes].astype(f32))
            design_ref[base + q, 0:8] = a8 * rows_ref[pl.ds(first + 8, 8), :]
            design_ref[base + q, 8:16] = a8 * rows_ref[pl.ds(first + 16, 8), :]
            hot_ref[base + q] = one_hot(rows_ref[pl.ds(first, 1), :], LANES)
            right_ref[group, here_lanes, 0:LANES] = one_hot(rows_ref[pl.ds(first + 1, 1), :], LANES).T
            right_ref[group, here_lanes, LANES:] = one_hot(rows_ref[pl.ds(first + 2, 1), :], LANES).T
            weight = spread(rows_ref, first + 3)
            sterm = sterm_ref[0, :, lanes].astype(f32)
            eight = jnp.concatenate([sterm[0:4], calib_in_ref[0, :, lanes].astype(f32)], axis=0)
            fifth = jnp.broadcast_to(sterm[4:5], (8, LANES))
            scaled = weight * eight
            scaled_fifth = jnp.where(rows == 0, weight * fifth, 0.0)
            scaled_ref[base + q, 0:8] = scaled
            scaled_ref[base + q, 8:16] = scaled_fifth
            high, rest = split_two(jnp.concatenate([scaled * eight, scaled_fifth * fifth], axis=0))
            lefts.append(jnp.concatenate([high, rest], axis=0))
        damp_acc[...] += jnp.dot(
            jnp.concatenate(lefts, axis=1), right_ref[group], preferred_element_type=f32
        )

    early = groups // 4
    middle = 3 * groups // 4
    loop(0, early, prepare)
    pl.semaphore_wait(barrier, owners + segments - 2)

    def pair_copy(k):
        target_chip = lax.rem(chip + k, chips)
        return pltpu.make_async_remote_copy(
            src_ref=parts_ref.at[1 - core, target_chip], dst_ref=got_pair.at[k],
            send_sem=pair_send.at[k], recv_sem=pair_recv.at[k],
            device_id={"src": partner}, device_id_type=MESH,
        )

    def chip_copy(k):
        return pltpu.make_async_remote_copy(
            src_ref=mine.at[k], dst_ref=got_chip.at[k],
            send_sem=chip_send.at[k], recv_sem=chip_recv.at[k],
            device_id={"src": 2 * lax.rem(chip + k, chips) + core}, device_id_type=MESH,
        )

    loop(1, chips, lambda k: pair_copy(k).start())
    pair_copy(0).start()

    def add_pair(k):
        pair_copy(k).wait_recv()
        mine[k] = parts_ref[core, lax.rem(chip + k, chips)] + got_pair[k]

    add_pair(1)

    def add_and_send(k):
        add_pair(k)
        chip_copy(k - 1).start()

    loop(2, chips, add_and_send)
    add_pair(0)
    chip_copy(chips - 1).start()
    loop(early, middle, prepare)

    def gather(k, total):
        chip_copy(k).wait_recv()
        return total + got_chip[k]

    total = lax.fori_loop(1, chips, gather, mine[0])
    step = solve_owner([total[8 * t : 8 * t + 8] for t in range(PACKED // 8)])
    got_step[me] = step[0:4]
    step_ref[0] = step[0:4]

    def step_copy(k, slot):
        return pltpu.make_async_remote_copy(
            src_ref=got_step.at[slot], dst_ref=got_step.at[slot],
            send_sem=step_send.at[k], recv_sem=step_recv.at[slot],
            device_id={"src": lax.rem(me + k, owners)}, device_id_type=MESH,
        )

    loop(1, owners, lambda k: step_copy(k, me).start())
    loop(middle, groups, prepare)

    def make_table(slot):
        x8 = twice(got_step[slot])
        table = jnp.concatenate(
            [
                jnp.where(low, x8, pltpu.roll(x8, LANES - 1, 1)),
                jnp.where(low, pltpu.roll(x8, LANES - 2, 1), pltpu.roll(x8, LANES - 3, 1)),
            ],
            axis=0,
        )
        high, rest = split_two(table)
        table_ref[slot] = jnp.concatenate([high, rest], axis=0)

    make_table(me)

    def arrive(k):
        slot = lax.rem(me + k, owners)
        step_copy(k, slot).wait_recv()
        make_table(slot)

    loop(1, owners, arrive)

    def correct(group):
        base = pl.multiple_of(group * GROUP, GROUP)
        lefts = []
        for q in range(GROUP):
            block = base + q
            values = jnp.dot(
                table_ref[owner_ref[block]], hot_ref[block], preferred_element_type=f32
            )
            term = design_ref[block, 0:8] * (values[0:8] + values[16:24]) + design_ref[
                block, 8:16
            ] * (values[8:16] + values[24:32])
            term = term + pltpu.roll(term, 4, 0)
            term = term + pltpu.roll(term, 2, 0)
            term = term + pltpu.roll(term, 1, 0)
            updated = spread(resid_ref, block) - term
            updated_ref[pl.ds(block, 1), :] = updated[0:1]
            high, rest = split_two(
                jnp.concatenate(
                    [updated * scaled_ref[block, 0:8], updated * scaled_ref[block, 8:16]], axis=0
                )
            )
            lefts.append(jnp.concatenate([high, rest], axis=0))
        pull_acc[...] += jnp.dot(
            jnp.concatenate(lefts, axis=1), right_ref[group], preferred_element_type=f32
        )

    loop(0, groups, correct)
    pull = pull_acc[0:16] + pull_acc[16:32]
    damp = damp_acc[0:16] + damp_acc[16:32]
    srcsum_ref[0:8] = jnp.concatenate([pull[0:4, 0:LANES], damp[0:4, 0:LANES]], axis=0)
    srcsum_ref[8:16] = pull[8:16, 0:LANES] + pltpu.roll(damp[8:16, 0:LANES], 1, 0)
    lane = lax.broadcasted_iota(jnp.int32, (8, LANES), 1)
    both = jnp.where(lane < 64, pull[0:8, LANES:], pltpu.roll(damp[0:8, LANES:], 64, 1))
    calsum_ref[...] = both[4:8]

    def src_copy(k, slot):
        return pltpu.make_async_remote_copy(
            src_ref=srcsum_ref, dst_ref=got_src.at[slot],
            send_sem=src_send.at[k], recv_sem=src_recv.at[slot],
            device_id={"seg": lax.rem(segment + k, segments)}, device_id_type=MESH,
        )

    def cal_copy(k, slot):
        return pltpu.make_async_remote_copy(
            src_ref=calsum_ref, dst_ref=got_cal.at[slot],
            send_sem=cal_send.at[k], recv_sem=cal_recv.at[slot],
            device_id={"src": lax.rem(me + k, owners)}, device_id_type=MESH,
        )

    got_src[segment] = srcsum_ref[...]
    got_cal[me] = calsum_ref[...]
    loop(1, segments, lambda k: src_copy(k, segment).start())
    loop(1, owners, lambda k: cal_copy(k, me).start())

    def drain(k):
        pair_copy(k).wait_send()
        chip_copy(k).wait_send()

    loop(1, chips, drain)
    pair_copy(0).wait_send()
    loop(1, owners, lambda k: step_copy(k, me).wait_send())
    loop(1, segments, lambda k: src_copy(k, lax.rem(segment + k, segments)).wait_recv())
    total = got_src[0]
    for k in range(1, segments):
        total = total + got_src[k]
    source_ref[0:4] = total[0:4] / (1.0 + total[4:8])
    source_ref[4:5] = total[8:9] / (1.0 + total[9:10])
    loop(1, owners, lambda k: cal_copy(k, lax.rem(me + k, owners)).wait_recv())
    total = got_cal[0]
    for k in range(1, owners):
        total = total + got_cal[k]
    result = total / (1.0 + pltpu.roll(total, 64, 1))
    calib_ref[0] = result[:, 0:CCDS]
    loop(1, segments, lambda k: src_copy(k, segment).wait_send())
    loop(1, owners, lambda k: cal_copy(k, me).wait_send())


def hand_out_kernel(*refs):
    for given, out in zip(refs[:4], refs[4:]):
        out[...] = given[...]


def body(
    attitude_partials, scan_phase, huber_weight, residual, knot_offset, detector_index,
    calibration_partials, source_index, source_partials, send_counts,
):
    owners = lax.axis_size("src")
    segments = lax.axis_size("seg")
    blocks = scan_phase.shape[1] // BSIZE
    capacity = 2 * blocks // owners
    chips = owners // 2
    spec = pl.BlockSpec(memory_space=VMEM)
    scalars = pl.BlockSpec(memory_space=pltpu.SMEM)
    shape = jax.ShapeDtypeStruct
    dma = pltpu.SemaphoreType.DMA

    def by_block(x):
        return x.reshape(blocks, BSIZE)

    phase, weight, resid, offset = map(by_block, (scan_phase, huber_weight, residual, knot_offset))
    parts, owner_of = pl.pallas_call(
        functools.partial(assemble_kernel, owners, capacity),
        out_shape=(shape((2, chips, PACKED, LANES), f32), shape((blocks + capacity,), jnp.int32)),
        in_specs=[scalars] + [spec] * 5,
        out_specs=(spec, scalars),
        scratch_shapes=[VMEM((GROUP * 64, LANES), f32), VMEM((owners, LANES, LANES), f32)],
        name="assemble",
    )(send_counts.reshape(1, owners), attitude_partials, phase, weight, resid, offset)
    results = (
        shape((1, 4, LANES), f32), shape((1, CALP, CCDS), f32), shape((SP, LANES), f32),
        shape((blocks, BSIZE), f32),
    )
    refined = pl.pallas_call(
        functools.partial(refine_kernel, owners, segments),
        out_shape=results,
        in_specs=[scalars] + [spec] * 10,
        out_specs=(spec,) * 4,
        scratch_shapes=[VMEM((chips, PACKED, LANES), f32)] * 3
        + [
            VMEM((owners, 4, LANES), f32), VMEM((GROUP * 24, LANES), f32),
            VMEM((owners, 32, LANES), bf16), VMEM((32, 2 * LANES), f32),
            VMEM((32, 2 * LANES), f32), VMEM((blocks, LANES, BSIZE), bf16),
            VMEM((blocks // GROUP, GROUP * BSIZE, 2 * LANES), bf16),
            VMEM((blocks, 16, BSIZE), f32), VMEM((blocks, 16, BSIZE), f32),
            VMEM((4, LANES), f32), VMEM((16, LANES), f32),
            VMEM((owners, 4, LANES), f32), VMEM((segments, 16, LANES), f32),
        ]
        + [dma((chips,))] * 4
        + [dma((owners,))] * 4
        + [dma((segments,))] * 2,
        compiler_params=pltpu.CompilerParams(
            collective_id=0, has_side_effects=True, vmem_limit_bytes=67043328
        ),
        name="refine",
    )(
        owner_of, parts, attitude_partials, phase, weight, resid, offset,
        by_block(detector_index), calibration_partials, by_block(source_index), source_partials,
    )
    step, calib, source, updated = pl.pallas_call(
        hand_out_kernel,
        out_shape=results,
        in_specs=[spec] * 4,
        out_specs=(spec,) * 4,
        name="hand_out",
    )(*refined)
    return (step, calib, source, updated.reshape(1, blocks * BSIZE))


def solution(mesh):
    return jax.shard_map(
        body,
        mesh=mesh,
        in_specs=(
            P("seg", None, "src"),
            P("seg", "src"),
            P("seg", "src"),
            P("seg", "src"),
            P("seg", "src"),
            P("seg", "src"),
            P("seg", None, "src"),
            P("seg", "src"),
            P("seg", None, "src"),
            P("seg", "src", None),
        ),
        out_specs=(P("seg", None, "src"), P("seg", None, None), P(None, "src"), P("seg", "src")),
        check_vma=False,
    )
```
